32 devices in a mesh: dom: 2 (over x), shard: 16 (over z, y, core).
Axes of the slice: x: 2, y: 2, z: 4, core: 2. Of those that a mesh axis runs over, the one named last changes fastest.
Arguments:
- activations: bfloat16 [4096, 8192], P(('dom', 'shard')), parts along dimension 0, may hold values from -6 to 6
- out_grads: bfloat16 [4096, 28672], P(('dom', 'shard')), parts along dimension 0, may hold values from -6 to 6
- example_ids: int32 [32, 128], P(('dom', 'shard')), parts along dimension 0, may hold values from 0 to 7, never falling along the last dimension, each value on 1 to 32 neighbouring positions
- in_factor: bfloat16 [64, 8192], P(None, 'shard'), may hold values from -0.0625 to 0.0625
- out_factor: bfloat16 [64, 28672], P(None, 'shard'), may hold values from -0.03125 to 0.03125
- query_grads: float32 [128, 4096], P('shard'), may hold values from -6 to 6
- basis_in: float32 [64, 64], replicated, may hold values from -0.75 to 0.75
- basis_out: float32 [64, 64], replicated, may hold values from -0.75 to 0.75
- eigen: float32 [64, 64], replicated, may hold values from 0.5 to 4
Outputs:
- scores: float32 [256, 128], P('dom', 'shard'), parts along dimension 0
The draws below stay inside these ranges and needn't reach their ends.
There are 2 independent parts, one for each index of `dom`. The reference program is written for one: setup_inputs(seed, part) draws one part's arguments, and reference() takes and returns one part's arrays. A program takes and returns all parts, laid end to end along the dimension named above; an argument that names none is the same for every part. Nothing has to cross between parts.
Inputs may be any that keep to these rules, and one draw needn't show every extreme that they name: `example_ids`: in each row (the 128 tokens of one shard) the example numbers never fall, and every number from 0 to 7 covers 1 to 32 tokens.
All inputs are finite; a program needn't handle non-finite values.
Results may differ from the reference program's by a relative error of at most 0.005.
Values may be sent and summed in bfloat16 or wider, within the bound.
A program may use at most 128 MiB of HBM per device.

```python
import math
import jax
import jax.numpy as jnp
import numpy as np
from jax import lax

D = 8192
FF = 28672
RANK = 64
TOK_DEV = 128
EX_DEV = 8
MOST = 32
TOKENS = 2048
QUERIES = 128
N_SHARD = 16


def block_scale(own_key, dims, pieces, smallest, top_value):
    loudness = 1.0
    for dim, shards_of in pieces:
        steps = jax.random.uniform(jax.random.fold_in(jax.random.fold_in(own_key, 6), dim), (shards_of,), jnp.float32, smallest / len(pieces), top_value / len(pieces))
        loudness = loudness * jnp.repeat(jnp.exp(steps), dims[dim] // shards_of).reshape((-1,) + (1,) * (len(dims) - 1 - dim))
    return loudness


def split_up(count, total, bound, skew):
    loads = [(1 << 20) // math.isqrt(standing ** skew) + 1 for standing in range(2, count + 1)]
    rest, counts = total - bound - (count - 1), [1] * (count - 1)
    while rest > 0:
        free = [i for i in range(count - 1) if counts[i] < bound]
        pool, budget = sum([loads[i] for i in free]), rest
        for i in free:
            extra = min(bound - counts[i], max(1, budget * loads[i] // pool), rest)
            counts[i] = counts[i] + extra
            rest = rest - extra
    return np.array([bound] + counts)


def ragged(stream_key, number_of, total, limit, lean):
    if number_of == 2:
        one = jax.random.randint(stream_key, (), max(1, total - limit), min(limit, total - 1) + 1)
        return jnp.stack([one, total - one])
    sizes = jnp.asarray(split_up(number_of, total, limit, lean), jnp.int32)
    twos = (number_of - 1) // 2
    donor, sink = sizes[1:1 + 2 * twos:2], sizes[2:2 + 2 * twos:2]
    room = jnp.minimum(donor - 1, limit - sink)
    shifted = jax.random.randint(jax.random.fold_in(stream_key, 1), (twos,), 0, 1 << 20) % (room + 1)
    sizes = sizes.at[1:1 + 2 * twos:2].set(donor - shifted).at[2:2 + 2 * twos:2].set(sink + shifted)
    return sizes[jax.random.permutation(jax.random.fold_in(stream_key, 2), number_of)]


def gaussian(rng, shape, deviation, limit, shards=(), kind=jnp.bfloat16):
    entries = jax.random.normal(rng, shape, jnp.float32) * deviation
    if len(shards) > 0:
        entries = block_scale(rng, shape, shards, -0.22, 0.18) * entries
    return jnp.clip(entries, min=-limit, max=limit).astype(kind)


def setup_inputs(seed: int = 0, part: int = 0) -> dict:
    splits = jax.random.split(jax.random.key(seed), 10)
    part_keys = jax.random.split(jax.random.fold_in(splits[9], part), 10)
    return {
        "activations": gaussian(part_keys[0], (TOKENS, D), 1.0, 6.0, ((0, 16),)),
        "out_grads": gaussian(part_keys[1], (TOKENS, FF), 1.0, 6.0, ((0, 16),)),
        "example_ids": jax.vmap(lambda own: jnp.searchsorted(jnp.cumsum(ragged(own, EX_DEV, TOK_DEV, MOST, 1)), jnp.arange(TOK_DEV), side="right"))(jax.random.split(part_keys[2], N_SHARD)).reshape((N_SHARD, TOK_DEV)).astype(jnp.int32),
        "in_factor": gaussian(splits[3], (RANK, D), D ** -0.5, 0.0625, ((1, 16),)),
        "out_factor": gaussian(splits[4], (RANK, FF), FF ** -0.5, 0.03125, ((1, 16),)),
        "query_grads": gaussian(splits[5], (QUERIES, RANK * RANK), 1.0, 6.0, ((0, 16),), jnp.float32),
        "basis_in": gaussian(splits[6], (RANK, RANK), RANK ** -0.5, 0.75, (), jnp.float32),
        "basis_out": gaussian(splits[7], (RANK, RANK), RANK ** -0.5, 0.75, (), jnp.float32),
        "eigen": jnp.clip(jnp.exp(jax.random.uniform(splits[8], (RANK, RANK), jnp.float32, math.log(0.5), math.log(4.0))), 0.5, 4.0),
    }


def per_example(proj_in, proj_out, ids, groups):
    member = (ids[None, :] == jnp.arange(groups, dtype=jnp.int32)[:, None]).astype(jnp.float32)
    weighted = member[:, :, None] * proj_in.astype(jnp.float32)[None, :, :]
    blocks = jnp.einsum("eti,tj->eij", weighted, proj_out.astype(jnp.float32), precision=lax.Precision.HIGHEST)
    return blocks.reshape(groups, -1)


def precondition(query_grads, basis_in, basis_out, eigen):
    rank = basis_in.shape[0]
    grads = query_grads.reshape(-1, rank, rank)
    rotated = jnp.einsum("ai,qab,bj->qij", basis_in, grads, basis_out, precision=lax.Precision.HIGHEST)
    scaled = rotated / eigen
    restored = jnp.einsum("ia,qab,jb->qij", basis_in, scaled, basis_out, precision=lax.Precision.HIGHEST)
    return restored.reshape(grads.shape[0], -1).astype(jnp.bfloat16)


def reference(activations, out_grads, example_ids, in_factor, out_factor, query_grads, basis_in, basis_out, eigen):
    feature_blocks = activations.reshape(N_SHARD, TOK_DEV, D)
    grad_blocks = out_grads.reshape(N_SHARD, TOK_DEV, FF)

    def one_shard(items):
        features, grads, ids = items
        proj_in = jnp.dot(features, in_factor.T, preferred_element_type=jnp.float32).astype(jnp.bfloat16)
        proj_out = jnp.dot(grads, out_factor.T, preferred_element_type=jnp.float32).astype(jnp.bfloat16)
        return per_example(proj_in, proj_out, ids, EX_DEV)

    example_grads = lax.map(one_shard, (feature_blocks, grad_blocks, example_ids))
    example_grads = example_grads.reshape(N_SHARD * EX_DEV, RANK * RANK)
    precond = precondition(query_grads, basis_in, basis_out, eigen)
    scores = jnp.dot(example_grads, precond.astype(jnp.float32).T, precision=lax.Precision.HIGHEST)
    return scores * 0.00390625
```

```python
import functools

import jax
import jax.numpy as jnp
from jax import lax
from jax.experimental import pallas as pl
from jax.experimental.pallas import tpu as pltpu
from jax.sharding import PartitionSpec as P

EX_DEV = 8
MESH = pl.DeviceIdType.MESH
HIGHEST = lax.Precision.HIGHEST
NT = (((1,), (1,)), ((), ()))
SCALE = 0.00390625
IDS = 16


def precondition(query_grads, basis_in, basis_out, eigen):
    rank = basis_in.shape[0]
    grads = query_grads.reshape(-1, rank, rank)
    rotated = jnp.einsum(
        "ai,qab,bj->qij", basis_in, grads, basis_out, precision=HIGHEST
    )
    scaled = rotated / eigen
    restored = jnp.einsum(
        "ia,qab,jb->qij", basis_in, scaled, basis_out, precision=HIGHEST
    )
    return restored.reshape(grads.shape[0], -1).astype(jnp.bfloat16)


def fold_columns(features, piece):
    return lax.dot_general(features, piece, NT, preferred_element_type=jnp.float32)


def with_collectives(
    activations,
    out_grads,
    example_ids,
    in_factor,
    out_factor,
    query_grads,
    basis_in,
    basis_out,
    eigen,
):
    rank = in_factor.shape[0]
    proj_in = fold_columns(
        activations, lax.all_gather(in_factor, "shard", axis=1, tiled=True)
    ).astype(jnp.bfloat16)
    proj_out = fold_columns(
        out_grads, lax.all_gather(out_factor, "shard", axis=1, tiled=True)
    ).astype(jnp.bfloat16)
    precond = precondition(query_grads, basis_in, basis_out, eigen)
    total_examples = EX_DEV * lax.axis_size("shard")
    global_ids = example_ids[0] + lax.axis_index("shard") * EX_DEV
    query_mats = precond.reshape(-1, rank, rank)
    rows_in = lax.all_gather(proj_in, "shard", axis=0, tiled=True)
    rows_out = lax.all_gather(proj_out, "shard", axis=0, tiled=True)
    owners = lax.all_gather(global_ids, "shard", axis=0, tiled=True)
    turned = jnp.einsum("ti,qij->tqj", rows_in, query_mats, preferred_element_type=jnp.float32)
    per_token = jnp.sum(turned * rows_out.astype(jnp.float32)[:, None, :], axis=2)
    scores = jax.ops.segment_sum(per_token, owners, num_segments=total_examples)
    return scores * SCALE


def pick(value, table):
    found = jnp.int32(table[0])
    for key in range(1, len(table)):
        found = jnp.where(value == key, jnp.int32(table[key]), found)
    return found


def kernel(
    lines,
    acts_hbm,
    grads_hbm,
    ids_ref,
    fin_hbm,
    fout_hbm,
    query_ref,
    bin_ref,
    bout_ref,
    eig_ref,
    out_ref,
    acts,
    grads,
    fin,
    fout,
    rin,
    rout,
    acc_in,
    acc_out,
    turned,
    mats,
    blocks,
    wide,
    load_sem,
    send_fin,
    send_fout,
    send_rin,
    send_rout,
    recv_fin,
    recv_fout,
    recv_rin,
    recv_rout,
):
    x = lax.axis_index("dom")
    s = lax.axis_index("shard")
    z, y, c = s // 4, (s // 2) % 2, s % 2
    rank = fin.shape[1]
    half = rank // 2
    quarter = rank // 4
    n_query = query_ref.shape[0]

    def place(zz, yy, cc):
        return (zz * 2 + yy) * 2 + cc

    up = jnp.minimum(z + 1, lines - 1)
    down = jnp.maximum(z - 1, 0)
    has_up, has_down = z < lines - 1, z > 0
    dev_up, dev_down = (x, place(up, y, c)), (x, place(down, y, c))
    dev_y, dev_x, dev_core = (x, place(z, 1 - y, c)), (1 - x, s), (x, place(z, y, 1 - c))

    loads = [
        pltpu.make_async_copy(fin_hbm, fin.at[s], load_sem.at[0]),
        pltpu.make_async_copy(fout_hbm, fout.at[s], load_sem.at[1]),
        pltpu.make_async_copy(acts_hbm, acts, load_sem.at[2]),
        pltpu.make_async_copy(grads_hbm, grads, load_sem.at[3]),
    ]
    for load in loads:
        load.start()

    barrier = pltpu.get_barrier_semaphore()

    def greet(dev):
        pl.semaphore_signal(barrier, inc=1, device_id=dev, device_id_type=MESH)

    @pl.when(has_up)
    def _():
        greet(dev_up)

    @pl.when(has_down)
    def _():
        greet(dev_down)

    greet(dev_y)
    greet(dev_x)
    greet(dev_core)
    pl.semaphore_wait(
        barrier, 3 + jnp.where(has_up, 1, 0) + jnp.where(has_down, 1, 0)
    )

    stores = (fin, fout, rin, rout)
    sends = (send_fin, send_fout, send_rin, send_rout)
    recvs = (recv_fin, recv_fout, recv_rin, recv_rout)
    pending = []

    def block(f, g):
        if f >= 2:
            return 0, 0, stores[f].shape[1]
        if g == "native":
            return x, pl.multiple_of(x * quarter, quarter), quarter
        if g == "cross":
            return 1 - x, pl.multiple_of((1 - x) * quarter, quarter), quarter
        return 2, half, half

    def copy(f, g, p, kind, dev):
        slot, start, size = block(f, g)
        ref = stores[f].at[p, pl.ds(start, size)]
        return pltpu.make_async_remote_copy(
            src_ref=ref,
            dst_ref=ref,
            send_sem=sends[f].at[kind, slot, p],
            recv_sem=recvs[f].at[slot, p],
            device_id=dev,
            device_id_type=MESH,
        )

    def send(f, g, p, kind, dev, cond=None):
        make = functools.partial(copy, f, g, p, kind, dev)
        if cond is None:
            make().start()
        else:

            @pl.when(cond)
            def _():
                make().start()

        pending.append((cond, make))

    def arrive(f, g, p):
        copy(f, g, p, 0, dev_core).wait_recv()

    def along(f, g, p, zz=None):
        if zz is None:
            send(f, g, p, 0, dev_up, has_up)
            send(f, g, p, 1, dev_down, has_down)
            return
        from_below = zz < z
        dev = (x, jnp.where(from_below, dev_up[1], dev_down[1]))
        cond = jnp.where(from_below, z + 1, lines - z) < lines
        send(f, g, p, 0, dev, cond)

    def yz_first(f, g):
        return f == 0 and g == "rest"

    def own(f):
        for g in ("native", "rest") if f < 2 else ("all",):
            along(f, g, s)
            send(f, g, s, 2, dev_y)
        for g in ("native", "cross", "rest") if f < 2 else ("all",):
            send(f, g, s, 4, dev_core)

    near = [
        sorted([w for w in range(lines) if w != v], key=lambda w: (abs(w - v), w))
        for v in range(lines)
    ]
    others = [pick(z, [near[v][k] for v in range(lines)]) for k in range(lines - 1)]
    route = [(None, True)]
    for far in others:
        route += [(far, False), (far, True)]

    def spot(k, cc):
        far, turn = route[k]
        return place(z if far is None else far, 1 - y if turn else y, cc)

    def native(f, k):
        far, turn = route[k]
        p = spot(k, c)
        for g in ("native", "rest") if f < 2 else ("all",):
            arrive(f, g, p)
            if yz_first(f, g):
                along(f, g, p, far)
            elif not turn:
                along(f, g, p, far)
                send(f, g, p, 2, dev_y)
            if g == "native":
                send(f, g, p, 3, dev_x)
            send(f, g, p, 4, dev_core)

    def fold(f, p):
        xs, acc = ((acts, acc_in), (grads, acc_out))[f]
        width = stores[f].shape[2]
        cols = pl.ds(pl.multiple_of(p * width, 128), width)
        acc[...] += fold_columns(stores[f][p], xs[:, cols])

    def cross(f, k):
        p = spot(k, c)
        arrive(f, "cross", p)
        send(f, "cross", p, 4, dev_core)
        fold(f, p)

    def partner(f, k):
        p = dev_core[1] if k < 0 else spot(k, 1 - c)
        for g in ("native", "cross", "rest") if f < 2 else ("all",):
            arrive(f, g, p)
        if f < 2:
            fold(f, p)

    def turn_rows(p):
        turned[p] = jnp.dot(
            mats[...], rin[p, pl.ds(0, rank), :], preferred_element_type=jnp.float32
        )

    def finish(p):
        rows = rout[p].astype(jnp.float32)
        prod = turned[p].reshape(n_query, rank, rows.shape[1]) * rows[None]
        per_token = jnp.sum(prod, axis=1)
        ids = rin[p, pl.ds(rank, IDS), :].astype(jnp.float32)[:EX_DEV]
        want = lax.broadcasted_iota(jnp.int32, ids.shape, 0).astype(jnp.float32)
        member = jnp.where(ids == want, 1.0, 0.0).astype(jnp.bfloat16)
        high = per_token.astype(jnp.bfloat16)
        low = (per_token - high.astype(jnp.float32)).astype(jnp.bfloat16)
        total = fold_columns(member, high) + fold_columns(member, low)
        out_ref[pl.ds(pl.multiple_of(p * EX_DEV, EX_DEV), EX_DEV), :] = total * SCALE

    loads[0].wait()
    own(0)
    loads[1].wait()
    own(1)

    acc_in[...] = jnp.zeros_like(acc_in)
    acc_out[...] = jnp.zeros_like(acc_out)
    ids = jnp.broadcast_to(ids_ref[...].astype(jnp.float32), (IDS, ids_ref.shape[1]))
    rin[s, pl.ds(rank, IDS), :] = ids.astype(jnp.bfloat16)

    for a in range(rank):
        blocks[a] = query_ref[:, a * rank : (a + 1) * rank]
    first = jnp.dot(
        blocks[...].reshape(rank * n_query, rank), bout_ref[...], precision=HIGHEST
    )
    blocks[...] = first.reshape(rank, n_query, rank)
    for q in range(n_query):
        wide[:, q * rank : (q + 1) * rank] = blocks[:, q, :]
    rotated = jnp.dot(bin_ref[...].T, wide[...], precision=HIGHEST)
    wide[...] = rotated / jnp.concatenate([eig_ref[...]] * n_query, axis=1)
    wide[...] = jnp.dot(bin_ref[...], wide[...], precision=HIGHEST)
    for q in range(n_query):
        mats[q * rank : (q + 1) * rank, :] = lax.dot_general(
            bout_ref[...], wide[:, q * rank : (q + 1) * rank], NT, precision=HIGHEST,
            preferred_element_type=jnp.float32,
        ).astype(jnp.bfloat16)

    steps = len(route)
    order = [(f, k) for f in range(2) for k in range(steps)]
    lag, slow = 2, 3
    done_in = None
    rows_at = None
    row_step = 0
    for i in range(len(order) + slow):
        if i < len(order):
            native(*order[i])
        if i == 1:
            loads[2].wait()
            fold(0, s)
            partner(0, -1)
        if i == steps + 1:
            loads[3].wait()
            fold(1, s)
            partner(1, -1)
        if 0 <= i - lag < len(order):
            cross(*order[i - lag])
        if 0 <= i - slow:
            partner(*order[i - slow])
            if order[i - slow] == (0, steps - 1):
                rin[s, pl.ds(0, rank), :] = acc_in[...].astype(jnp.bfloat16)
                own(2)
                turn_rows(s)
                rows_at = i
        if rows_at is not None and i > rows_at and row_step < steps:
            native(2, row_step)
            turn_rows(spot(row_step, c))
            row_step += 1
    rout[s] = acc_out[...].astype(jnp.bfloat16)
    own(3)
    while row_step < steps:
        native(2, row_step)
        turn_rows(spot(row_step, c))
        row_step += 1
    for k in range(-1, steps):
        partner(2, k)
        turn_rows(dev_core[1] if k < 0 else spot(k, 1 - c))
    finish(s)
    partner(3, -1)
    finish(dev_core[1])
    for k in range(steps):
        native(3, k)
        finish(spot(k, c))
    for k in range(steps):
        partner(3, k)
        finish(spot(k, 1 - c))

    for cond, make in pending:
        if cond is None:
            make().wait_send()
        else:

            @pl.when(cond)
            def _(make=make):
                make().wait_send()


def in_one_kernel(
    activations,
    out_grads,
    example_ids,
    in_factor,
    out_factor,
    query_grads,
    basis_in,
    basis_out,
    eigen,
):
    n = lax.axis_size("shard")
    rank = in_factor.shape[0]
    tokens = activations.shape[0]
    n_query = query_grads.shape[0]
    bf16, f32 = jnp.bfloat16, jnp.float32
    hbm = pl.BlockSpec(memory_space=pl.ANY)
    vmem = pl.BlockSpec(memory_space=pltpu.VMEM)
    dma = pltpu.SemaphoreType.DMA
    return pl.pallas_call(
        functools.partial(kernel, n // 4),
        out_shape=jax.ShapeDtypeStruct((n * EX_DEV, n_query), f32),
        in_specs=[hbm, hbm, vmem, hbm, hbm, vmem, vmem, vmem, vmem],
        out_specs=vmem,
        scratch_shapes=[
            pltpu.VMEM(activations.shape, bf16),
            pltpu.VMEM(out_grads.shape, bf16),
            pltpu.VMEM((n,) + in_factor.shape, bf16),
            pltpu.VMEM((n,) + out_factor.shape, bf16),
            pltpu.VMEM((n, rank + IDS, tokens), bf16),
            pltpu.VMEM((n, rank, tokens), bf16),
            pltpu.VMEM((rank, tokens), f32),
            pltpu.VMEM((rank, tokens), f32),
            pltpu.VMEM((n, n_query * rank, tokens), f32),
            pltpu.VMEM((n_query * rank, rank), bf16),
            pltpu.VMEM((rank, n_query, rank), f32),
            pltpu.VMEM((rank, n_query * rank), f32),
            dma((4,)),
            dma((5, 3, n)),
            dma((5, 3, n)),
            dma((5, 1, n)),
            dma((5, 1, n)),
            dma((3, n)),
            dma((3, n)),
            dma((1, n)),
            dma((1, n)),
        ],
        compiler_params=pltpu.CompilerParams(collective_id=0, has_side_effects=True),
    )(
        activations,
        out_grads,
        example_ids,
        in_factor,
        out_factor,
        query_grads,
        basis_in,
        basis_out,
        eigen,
    )


def solution(mesh):
    placed = (
        P(("dom", "shard"), None),
        P(("dom", "shard"), None),
        P(("dom", "shard"), None),
        P(None, "shard"),
        P(None, "shard"),
        P("shard", None),
        P(),
        P(),
        P(),
    )
    small = mesh.shape["dom"] == 2 and mesh.shape["shard"] in (8, 16)
    return jax.shard_map(
        in_one_kernel if small else with_collectives,
        mesh=mesh,
        in_specs=placed,
        out_specs=P("dom", "shard"),
        check_vma=False,
    )
```

```python
import functools

import jax
import jax.numpy as jnp
from jax import lax
from jax.experimental import pallas as pl
from jax.experimental.pallas import tpu as pltpu
from jax.sharding import PartitionSpec as P

EX_DEV = 8
MESH = pl.DeviceIdType.MESH
HIGHEST = lax.Precision.HIGHEST
NT = (((1,), (1,)), ((), ()))
SCALE = 0.00390625
IDS = 16


def precondition(query_grads, basis_in, basis_out, eigen):
    rank = basis_in.shape[0]
    grads = query_grads.reshape(-1, rank, rank)
    rotated = jnp.einsum(
        "ai,qab,bj->qij", basis_in, grads, basis_out, precision=HIGHEST
    )
    scaled = rotated / eigen
    restored = jnp.einsum(
        "ia,qab,jb->qij", basis_in, scaled, basis_out, precision=HIGHEST
    )
    return restored.reshape(grads.shape[0], -1).astype(jnp.bfloat16)


def fold_columns(features, piece):
    return lax.dot_general(features, piece, NT, preferred_element_type=jnp.float32)


def with_collectives(
    activations,
    out_grads,
    example_ids,
    in_factor,
    out_factor,
    query_grads,
    basis_in,
    basis_out,
    eigen,
):
    rank = in_factor.shape[0]
    proj_in = fold_columns(
        activations, lax.all_gather(in_factor, "shard", axis=1, tiled=True)
    ).astype(jnp.bfloat16)
    proj_out = fold_columns(
        out_grads, lax.all_gather(out_factor, "shard", axis=1, tiled=True)
    ).astype(jnp.bfloat16)
    precond = precondition(query_grads, basis_in, basis_out, eigen)
    total_examples = EX_DEV * lax.axis_size("shard")
    global_ids = example_ids[0] + lax.axis_index("shard") * EX_DEV
    query_mats = precond.reshape(-1, rank, rank)
    rows_in = lax.all_gather(proj_in, "shard", axis=0, tiled=True)
    rows_out = lax.all_gather(proj_out, "shard", axis=0, tiled=True)
    owners = lax.all_gather(global_ids, "shard", axis=0, tiled=True)
    turned = jnp.einsum("ti,qij->tqj", rows_in, query_mats, preferred_element_type=jnp.float32)
    per_token = jnp.sum(turned * rows_out.astype(jnp.float32)[:, None, :], axis=2)
    scores = jax.ops.segment_sum(per_token, owners, num_segments=total_examples)
    return scores * SCALE


def pick(value, table):
    found = jnp.int32(table[0])
    for key in range(1, len(table)):
        found = jnp.where(value == key, jnp.int32(table[key]), found)
    return found


def kernel(
    lines,
    acts_hbm,
    grads_hbm,
    ids_ref,
    fin_hbm,
    fout_hbm,
    query_ref,
    bin_ref,
    bout_ref,
    eig_ref,
    out_ref,
    acts,
    grads,
    fin,
    fout,
    rin,
    rout,
    acc_in,
    acc_out,
    turned,
    mats,
    blocks,
    wide,
    load_sem,
    send_fin,
    send_fout,
    send_rin,
    send_rout,
    recv_fin,
    recv_fout,
    recv_rin,
    recv_rout,
):
    x = lax.axis_index("dom")
    s = lax.axis_index("shard")
    z, y, c = s // 4, (s // 2) % 2, s % 2
    rank = fin.shape[1]
    half = rank // 2
    quarter = rank // 4
    n_query = query_ref.shape[0]

    def place(zz, yy, cc):
        return (zz * 2 + yy) * 2 + cc

    up = jnp.minimum(z + 1, lines - 1)
    down = jnp.maximum(z - 1, 0)
    has_up, has_down = z < lines - 1, z > 0
    dev_up, dev_down = (x, place(up, y, c)), (x, place(down, y, c))
    dev_y, dev_x, dev_core = (x, place(z, 1 - y, c)), (1 - x, s), (x, place(z, y, 1 - c))

    loads = [
        pltpu.make_async_copy(fin_hbm, fin.at[s], load_sem.at[0]),
        pltpu.make_async_copy(fout_hbm, fout.at[s], load_sem.at[1]),
        pltpu.make_async_copy(acts_hbm, acts, load_sem.at[2]),
        pltpu.make_async_copy(grads_hbm, grads, load_sem.at[3]),
    ]
    for load in loads:
        load.start()

    barrier = pltpu.get_barrier_semaphore()

    def greet(dev):
        pl.semaphore_signal(barrier, inc=1, device_id=dev, device_id_type=MESH)

    @pl.when(has_up)
    def _():
        greet(dev_up)

    @pl.when(has_down)
    def _():
        greet(dev_down)

    greet(dev_y)
    greet(dev_x)
    greet(dev_core)
    pl.semaphore_wait(
        barrier, 3 + jnp.where(has_up, 1, 0) + jnp.where(has_down, 1, 0)
    )

    stores = (fin, fout, rin, rout)
    sends = (send_fin, send_fout, send_rin, send_rout)
    recvs = (recv_fin, recv_fout, recv_rin, recv_rout)
    pending = []

    def block(f, g):
        if f >= 2:
            return 0, 0, stores[f].shape[1]
        if g == "native":
            return x, pl.multiple_of(x * quarter, quarter), quarter
        if g == "cross":
            return 1 - x, pl.multiple_of((1 - x) * quarter, quarter), quarter
        return 2, half, half

    def copy(f, g, p, kind, dev):
        slot, start, size = block(f, g)
        ref = stores[f].at[p, pl.ds(start, size)]
        return pltpu.make_async_remote_copy(
            src_ref=ref,
            dst_ref=ref,
            send_sem=sends[f].at[kind, slot, p],
            recv_sem=recvs[f].at[slot, p],
            device_id=dev,
            device_id_type=MESH,
        )

    def send(f, g, p, kind, dev, cond=None):
        make = functools.partial(copy, f, g, p, kind, dev)
        if cond is None:
            make().start()
        else:

            @pl.when(cond)
            def _():
                make().start()

        pending.append((cond, make))

    def arrive(f, g, p):
        copy(f, g, p, 0, dev_core).wait_recv()

    def along(f, g, p, zz=None):
        if zz is None:
            send(f, g, p, 0, dev_up, has_up)
            send(f, g, p, 1, dev_down, has_down)
            return
        from_below = zz < z
        dev = (x, jnp.where(from_below, dev_up[1], dev_down[1]))
        cond = jnp.where(from_below, z + 1, lines - z) < lines
        send(f, g, p, 0, dev, cond)

    def yz_first(f, g):
        return f == 0 and g == "rest"

    def own(f):
        for g in ("native", "rest"):
            along(f, g, s)
            send(f, g, s, 2, dev_y)
        for g in ("native", "cross", "rest"):
            send(f, g, s, 4, dev_core)

    near = [
        sorted([w for w in range(lines) if w != v], key=lambda w: (abs(w - v), w))
        for v in range(lines)
    ]
    others = [pick(z, [near[v][k] for v in range(lines)]) for k in range(lines - 1)]
    route = [(None, True)]
    for far in others:
        route += [(far, False), (far, True)]

    def spot(k, cc):
        far, turn = route[k]
        return place(z if far is None else far, 1 - y if turn else y, cc)

    def spread(f):
        for k in reversed(range(len(route))):
            send(f, "all", s, k, (x, spot(k, c)))
        send(f, "all", s, len(route), dev_core)

    def passed(f, k):
        p = spot(k, c)
        arrive(f, "all", p)
        send(f, "all", p, len(route), dev_core)

    def native(f, k):
        far, turn = route[k]
        p = spot(k, c)
        for g in ("native", "rest"):
            arrive(f, g, p)
            if yz_first(f, g):
                along(f, g, p, far)
            elif not turn:
                along(f, g, p, far)
                send(f, g, p, 2, dev_y)
            if g == "native":
                send(f, g, p, 3, dev_x)
            send(f, g, p, 4, dev_core)

    def fold(f, p):
        xs, acc = ((acts, acc_in), (grads, acc_out))[f]
        width = stores[f].shape[2]
        cols = pl.ds(pl.multiple_of(p * width, 128), width)
        acc[...] += fold_columns(stores[f][p], xs[:, cols])

    def cross(f, k):
        p = spot(k, c)
        arrive(f, "cross", p)
        send(f, "cross", p, 4, dev_core)
        fold(f, p)

    def partner(f, k):
        p = dev_core[1] if k < 0 else spot(k, 1 - c)
        for g in ("native", "cross", "rest"):
            arrive(f, g, p)
        fold(f, p)

    def turn_rows(p):
        turned[p] = jnp.dot(
            mats[...], rin[p, pl.ds(0, rank), :], preferred_element_type=jnp.float32
        )

    def finish(p):
        rows = rout[p].astype(jnp.float32)
        prod = turned[p].reshape(n_query, rank, rows.shape[1]) * rows[None]
        per_token = jnp.sum(prod, axis=1)
        ids = rin[p, pl.ds(rank, IDS), :].astype(jnp.float32)[:EX_DEV]
        want = lax.broadcasted_iota(jnp.int32, ids.shape, 0).astype(jnp.float32)
        member = jnp.where(ids == want, 1.0, 0.0).astype(jnp.bfloat16)
        high = per_token.astype(jnp.bfloat16)
        low = (per_token - high.astype(jnp.float32)).astype(jnp.bfloat16)
        total = fold_columns(member, high) + fold_columns(member, low)
        out_ref[pl.ds(pl.multiple_of(p * EX_DEV, EX_DEV), EX_DEV), :] = total * SCALE

    loads[0].wait()
    own(0)
    loads[1].wait()
    own(1)

    acc_in[...] = jnp.zeros_like(acc_in)
    acc_out[...] = jnp.zeros_like(acc_out)
    ids = jnp.broadcast_to(ids_ref[...].astype(jnp.float32), (IDS, ids_ref.shape[1]))
    rin[s, pl.ds(rank, IDS), :] = ids.astype(jnp.bfloat16)

    for a in range(rank):
        blocks[a] = query_ref[:, a * rank : (a + 1) * rank]
    first = jnp.dot(
        blocks[...].reshape(rank * n_query, rank), bout_ref[...], precision=HIGHEST
    )
    blocks[...] = first.reshape(rank, n_query, rank)
    for q in range(n_query):
        wide[:, q * rank : (q + 1) * rank] = blocks[:, q, :]
    rotated = jnp.dot(bin_ref[...].T, wide[...], precision=HIGHEST)
    wide[...] = rotated / jnp.concatenate([eig_ref[...]] * n_query, axis=1)
    wide[...] = jnp.dot(bin_ref[...], wide[...], precision=HIGHEST)
    for q in range(n_query):
        mats[q * rank : (q + 1) * rank, :] = lax.dot_general(
            bout_ref[...], wide[:, q * rank : (q + 1) * rank], NT, precision=HIGHEST,
            preferred_element_type=jnp.float32,
        ).astype(jnp.bfloat16)

    steps = len(route)
    lead, lag, slow = 3, 3, 4
    order = []
    for k in range(steps + lead):
        if k < steps:
            order.append((0, k))
        if k >= lead:
            order.append((1, k - lead))
    fold_own = {2: 0, 6: 1}

    def close(f, k):
        partner(f, k)
        if (f, k) == (0, steps - 1):
            rin[s, pl.ds(0, rank), :] = acc_in[...].astype(jnp.bfloat16)
            spread(2)

    for i in range(len(order)):
        native(*order[i])
        if i in fold_own:
            f = fold_own[i]
            loads[2 + f].wait()
            fold(f, s)
            partner(f, -1)
        if i >= lag:
            cross(*order[i - lag])
        if i >= slow:
            close(*order[i - slow])
    turn_rows(s)
    for k in range(steps):
        passed(2, k)
        turn_rows(spot(k, c))
    for i in range(len(order), len(order) + slow):
        if i - lag < len(order):
            cross(*order[i - lag])
        close(*order[i - slow])
    rout[s] = acc_out[...].astype(jnp.bfloat16)
    spread(3)
    for k in range(-1, steps):
        p = dev_core[1] if k < 0 else spot(k, 1 - c)
        arrive(2, "all", p)
        turn_rows(p)
    finish(s)
    arrive(3, "all", dev_core[1])
    finish(dev_core[1])
    for k in range(steps):
        passed(3, k)
        finish(spot(k, c))
    for k in range(steps):
        arrive(3, "all", spot(k, 1 - c))
        finish(spot(k, 1 - c))

    for cond, make in pending:
        if cond is None:
            make().wait_send()
        else:

            @pl.when(cond)
            def _(make=make):
                make().wait_send()


def in_one_kernel(
    activations,
    out_grads,
    example_ids,
    in_factor,
    out_factor,
    query_grads,
    basis_in,
    basis_out,
    eigen,
):
    n = lax.axis_size("shard")
    rank = in_factor.shape[0]
    tokens = activations.shape[0]
    n_query = query_grads.shape[0]
    bf16, f32 = jnp.bfloat16, jnp.float32
    hbm = pl.BlockSpec(memory_space=pl.ANY)
    vmem = pl.BlockSpec(memory_space=pltpu.VMEM)
    dma = pltpu.SemaphoreType.DMA
    return pl.pallas_call(
        functools.partial(kernel, n // 4),
        out_shape=jax.ShapeDtypeStruct((n * EX_DEV, n_query), f32),
        in_specs=[hbm, hbm, vmem, hbm, hbm, vmem, vmem, vmem, vmem],
        out_specs=vmem,
        scratch_shapes=[
            pltpu.VMEM(activations.shape, bf16),
            pltpu.VMEM(out_grads.shape, bf16),
            pltpu.VMEM((n,) + in_factor.shape, bf16),
            pltpu.VMEM((n,) + out_factor.shape, bf16),
            pltpu.VMEM((n, rank + IDS, tokens), bf16),
            pltpu.VMEM((n, rank, tokens), bf16),
            pltpu.VMEM((rank, tokens), f32),
            pltpu.VMEM((rank, tokens), f32),
            pltpu.VMEM((n, n_query * rank, tokens), f32),
            pltpu.VMEM((n_query * rank, rank), bf16),
            pltpu.VMEM((rank, n_query, rank), f32),
            pltpu.VMEM((rank, n_query * rank), f32),
            dma((4,)),
            dma((5, 3, n)),
            dma((5, 3, n)),
            dma((n // 2, 1, n)),
            dma((n // 2, 1, n)),
            dma((3, n)),
            dma((3, n)),
            dma((1, n)),
            dma((1, n)),
        ],
        compiler_params=pltpu.CompilerParams(collective_id=0, has_side_effects=True),
    )(
        activations,
        out_grads,
        example_ids,
        in_factor,
        out_factor,
        query_grads,
        basis_in,
        basis_out,
        eigen,
    )


def solution(mesh):
    placed = (
        P(("dom", "shard"), None),
        P(("dom", "shard"), None),
        P(("dom", "shard"), None),
        P(None, "shard"),
        P(None, "shard"),
        P("shard", None),
        P(),
        P(),
        P(),
    )
    small = mesh.shape["dom"] == 2 and mesh.shape["shard"] in (8, 16)
    return jax.shard_map(
        in_one_kernel if small else with_collectives,
        mesh=mesh,
        in_specs=placed,
        out_specs=P("dom", "shard"),
        check_vma=False,
    )
```

```python
import functools

import jax
import jax.numpy as jnp
from jax import lax
from jax.experimental import pallas as pl
from jax.experimental.pallas import tpu as pltpu
from jax.sharding import PartitionSpec as P

EX_DEV = 8
MESH = pl.DeviceIdType.MESH
HIGHEST = lax.Precision.HIGHEST
NT = (((1,), (1,)), ((), ()))
SCALE = 0.00390625
IDS = 16


def precondition(query_grads, basis_in, basis_out, eigen):
    rank = basis_in.shape[0]
    grads = query_grads.reshape(-1, rank, rank)
    rotated = jnp.einsum(
        "ai,qab,bj->qij", basis_in, grads, basis_out, precision=HIGHEST
    )
    scaled = rotated / eigen
    restored = jnp.einsum(
        "ia,qab,jb->qij", basis_in, scaled, basis_out, precision=HIGHEST
    )
    return restored.reshape(grads.shape[0], -1).astype(jnp.bfloat16)


def fold_columns(features, piece):
    return lax.dot_general(features, piece, NT, preferred_element_type=jnp.float32)


def with_collectives(
    activations,
    out_grads,
    example_ids,
    in_factor,
    out_factor,
    query_grads,
    basis_in,
    basis_out,
    eigen,
):
    rank = in_factor.shape[0]
    proj_in = fold_columns(
        activations, lax.all_gather(in_factor, "shard", axis=1, tiled=True)
    ).astype(jnp.bfloat16)
    proj_out = fold_columns(
        out_grads, lax.all_gather(out_factor, "shard", axis=1, tiled=True)
    ).astype(jnp.bfloat16)
    precond = precondition(query_grads, basis_in, basis_out, eigen)
    total_examples = EX_DEV * lax.axis_size("shard")
    global_ids = example_ids[0] + lax.axis_index("shard") * EX_DEV
    query_mats = precond.reshape(-1, rank, rank)
    rows_in = lax.all_gather(proj_in, "shard", axis=0, tiled=True)
    rows_out = lax.all_gather(proj_out, "shard", axis=0, tiled=True)
    owners = lax.all_gather(global_ids, "shard", axis=0, tiled=True)
    turned = jnp.einsum("ti,qij->tqj", rows_in, query_mats, preferred_element_type=jnp.float32)
    per_token = jnp.sum(turned * rows_out.astype(jnp.float32)[:, None, :], axis=2)
    scores = jax.ops.segment_sum(per_token, owners, num_segments=total_examples)
    return scores * SCALE


def pick(value, table):
    found = jnp.int32(table[0])
    for key in range(1, len(table)):
        found = jnp.where(value == key, jnp.int32(table[key]), found)
    return found


def kernel(
    lines,
    acts_hbm,
    grads_hbm,
    ids_ref,
    fin_hbm,
    fout_hbm,
    query_ref,
    bin_ref,
    bout_ref,
    eig_ref,
    out_ref,
    acts,
    grads,
    fin,
    fout,
    rin,
    rout,
    acc_in,
    acc_out,
    turned,
    mats,
    blocks,
    wide,
    load_sem,
    send_fin,
    send_fout,
    send_rin,
    send_rout,
    recv_fin,
    recv_fout,
    recv_rin,
    recv_rout,
):
    x = lax.axis_index("dom")
    s = lax.axis_index("shard")
    z, y, c = s // 4, (s // 2) % 2, s % 2
    rank = fin.shape[1]
    half = rank // 2
    quarter = rank // 4
    n_query = query_ref.shape[0]

    def place(zz, yy, cc):
        return (zz * 2 + yy) * 2 + cc

    up = jnp.minimum(z + 1, lines - 1)
    down = jnp.maximum(z - 1, 0)
    has_up, has_down = z < lines - 1, z > 0
    dev_up, dev_down = (x, place(up, y, c)), (x, place(down, y, c))
    dev_y, dev_x, dev_core = (x, place(z, 1 - y, c)), (1 - x, s), (x, place(z, y, 1 - c))

    loads = [
        pltpu.make_async_copy(fin_hbm, fin.at[s], load_sem.at[0]),
        pltpu.make_async_copy(fout_hbm, fout.at[s], load_sem.at[1]),
        pltpu.make_async_copy(acts_hbm, acts, load_sem.at[2]),
        pltpu.make_async_copy(grads_hbm, grads, load_sem.at[3]),
    ]
    for load in loads:
        load.start()

    barrier = pltpu.get_barrier_semaphore()

    def greet(dev):
        pl.semaphore_signal(barrier, inc=1, device_id=dev, device_id_type=MESH)

    @pl.when(has_up)
    def _():
        greet(dev_up)

    @pl.when(has_down)
    def _():
        greet(dev_down)

    greet(dev_y)
    greet(dev_x)
    greet(dev_core)
    pl.semaphore_wait(
        barrier, 3 + jnp.where(has_up, 1, 0) + jnp.where(has_down, 1, 0)
    )

    stores = (fin, fout, rin, rout)
    sends = (send_fin, send_fout, send_rin, send_rout)
    recvs = (recv_fin, recv_fout, recv_rin, recv_rout)
    pending = []

    def block(f, g):
        if f >= 2:
            return 0, 0, stores[f].shape[1]
        if g == "native":
            return x, pl.multiple_of(x * quarter, quarter), quarter
        if g == "cross":
            return 1 - x, pl.multiple_of((1 - x) * quarter, quarter), quarter
        return 2, half, half

    def copy(f, g, p, kind, dev):
        slot, start, size = block(f, g)
        ref = stores[f].at[p, pl.ds(start, size)]
        return pltpu.make_async_remote_copy(
            src_ref=ref,
            dst_ref=ref,
            send_sem=sends[f].at[kind, slot, p],
            recv_sem=recvs[f].at[slot, p],
            device_id=dev,
            device_id_type=MESH,
        )

    def send(f, g, p, kind, dev, cond=None):
        make = functools.partial(copy, f, g, p, kind, dev)
        if cond is None:
            make().start()
        else:

            @pl.when(cond)
            def _():
                make().start()

        pending.append((cond, make))

    def arrive(f, g, p):
        copy(f, g, p, 0, dev_core).wait_recv()

    def along(f, g, p, zz=None):
        if zz is None:
            send(f, g, p, 0, dev_up, has_up)
            send(f, g, p, 1, dev_down, has_down)
            return
        from_below = zz < z
        dev = (x, jnp.where(from_below, dev_up[1], dev_down[1]))
        cond = jnp.where(from_below, z + 1, lines - z) < lines
        send(f, g, p, 0, dev, cond)

    def yz_first(f, g):
        return f == 0 and g == "rest"

    def own(f):
        for g in ("native", "rest"):
            along(f, g, s)
            send(f, g, s, 2, dev_y)
        for g in ("native", "cross", "rest"):
            send(f, g, s, 4, dev_core)

    near = [
        sorted([w for w in range(lines) if w != v], key=lambda w: (abs(w - v), w))
        for v in range(lines)
    ]
    others = [pick(z, [near[v][k] for v in range(lines)]) for k in range(lines - 1)]
    route = [(None, True)]
    for far in others:
        route += [(far, False), (far, True)]

    def spot(k, cc):
        far, turn = route[k]
        return place(z if far is None else far, 1 - y if turn else y, cc)

    def spread(f):
        for k in reversed(range(len(route))):
            send(f, "all", s, k, (x, spot(k, c)))
        send(f, "all", s, len(route), dev_core)

    def passed(f, k):
        p = spot(k, c)
        arrive(f, "all", p)
        send(f, "all", p, len(route), dev_core)

    def native(f, k):
        far, turn = route[k]
        p = spot(k, c)
        for g in ("native", "rest"):
            arrive(f, g, p)
            if yz_first(f, g):
                along(f, g, p, far)
            elif not turn:
                along(f, g, p, far)
                send(f, g, p, 2, dev_y)
            if g == "native":
                send(f, g, p, 3, dev_x)
            send(f, g, p, 4, dev_core)

    def fold(f, p):
        xs, acc = ((acts, acc_in), (grads, acc_out))[f]
        width = stores[f].shape[2]
        cols = pl.ds(pl.multiple_of(p * width, 128), width)
        acc[...] += fold_columns(stores[f][p], xs[:, cols])

    def cross(f, k):
        p = spot(k, c)
        arrive(f, "cross", p)
        send(f, "cross", p, 4, dev_core)
        fold(f, p)

    def partner(f, k):
        p = dev_core[1] if k < 0 else spot(k, 1 - c)
        for g in ("native", "cross", "rest"):
            arrive(f, g, p)
        fold(f, p)

    def turn_rows(p):
        turned[p] = jnp.dot(
            mats[...], rin[p, pl.ds(0, rank), :], preferred_element_type=jnp.float32
        )

    def finish(p):
        rows = rout[p].astype(jnp.float32)
        prod = turned[p].reshape(n_query, rank, rows.shape[1]) * rows[None]
        per_token = jnp.sum(prod, axis=1)
        ids = rin[p, pl.ds(rank, IDS), :].astype(jnp.float32)[:EX_DEV]
        want = lax.broadcasted_iota(jnp.int32, ids.shape, 0).astype(jnp.float32)
        member = jnp.where(ids == want, 1.0, 0.0).astype(jnp.bfloat16)
        high = per_token.astype(jnp.bfloat16)
        low = (per_token - high.astype(jnp.float32)).astype(jnp.bfloat16)
        total = fold_columns(member, high) + fold_columns(member, low)
        out_ref[pl.ds(pl.multiple_of(p * EX_DEV, EX_DEV), EX_DEV), :] = total * SCALE

    loads[0].wait()
    own(0)
    loads[1].wait()
    own(1)

    acc_in[...] = jnp.zeros_like(acc_in)
    acc_out[...] = jnp.zeros_like(acc_out)
    ids = jnp.broadcast_to(ids_ref[...].astype(jnp.float32), (IDS, ids_ref.shape[1]))
    rin[s, pl.ds(rank, IDS), :] = ids.astype(jnp.bfloat16)

    for a in range(rank):
        blocks[a] = query_ref[:, a * rank : (a + 1) * rank]
    first = jnp.dot(
        blocks[...].reshape(rank * n_query, rank), bout_ref[...], precision=HIGHEST
    )
    blocks[...] = first.reshape(rank, n_query, rank)
    for q in range(n_query):
        wide[:, q * rank : (q + 1) * rank] = blocks[:, q, :]
    rotated = jnp.dot(bin_ref[...].T, wide[...], precision=HIGHEST)
    wide[...] = rotated / jnp.concatenate([eig_ref[...]] * n_query, axis=1)
    wide[...] = jnp.dot(bin_ref[...], wide[...], precision=HIGHEST)
    for q in range(n_query):
        mats[q * rank : (q + 1) * rank, :] = lax.dot_general(
            bout_ref[...], wide[:, q * rank : (q + 1) * rank], NT, precision=HIGHEST,
            preferred_element_type=jnp.float32,
        ).astype(jnp.bfloat16)

    steps = len(route)
    lead, lag, slow = 1, 4, 8
    order = []
    for k in range(steps + lead):
        if k < steps:
            order.append((0, k))
        if k >= lead:
            order.append((1, k - lead))
    fold_own = {2: 0, 6: 1}

    def close(f, k):
        partner(f, k)
        if (f, k) == (0, steps - 1):
            rin[s, pl.ds(0, rank), :] = acc_in[...].astype(jnp.bfloat16)
            spread(2)

    for i in range(len(order)):
        native(*order[i])
        if i in fold_own:
            f = fold_own[i]
            loads[2 + f].wait()
            fold(f, s)
            partner(f, -1)
        if i >= lag:
            cross(*order[i - lag])
        if i >= slow:
            close(*order[i - slow])
    for i in range(len(order), len(order) + slow):
        if i - lag < len(order):
            cross(*order[i - lag])
        close(*order[i - slow])
    rout[s] = acc_out[...].astype(jnp.bfloat16)
    spread(3)
    turn_rows(s)
    for k in range(steps):
        passed(2, k)
        turn_rows(spot(k, c))
    for k in range(-1, steps):
        p = dev_core[1] if k < 0 else spot(k, 1 - c)
        arrive(2, "all", p)
        turn_rows(p)
    finish(s)
    arrive(3, "all", dev_core[1])
    finish(dev_core[1])
    for k in range(steps):
        passed(3, k)
        finish(spot(k, c))
    for k in range(steps):
        arrive(3, "all", spot(k, 1 - c))
        finish(spot(k, 1 - c))

    for cond, make in pending:
        if cond is None:
            make().wait_send()
        else:

            @pl.when(cond)
            def _(make=make):
                make().wait_send()


def in_one_kernel(
    activations,
    out_grads,
    example_ids,
    in_factor,
    out_factor,
    query_grads,
    basis_in,
    basis_out,
    eigen,
):
    n = lax.axis_size("shard")
    rank = in_factor.shape[0]
    tokens = activations.shape[0]
    n_query = query_grads.shape[0]
    bf16, f32 = jnp.bfloat16, jnp.float32
    hbm = pl.BlockSpec(memory_space=pl.ANY)
    vmem = pl.BlockSpec(memory_space=pltpu.VMEM)
    dma = pltpu.SemaphoreType.DMA
    return pl.pallas_call(
        functools.partial(kernel, n // 4),
        out_shape=jax.ShapeDtypeStruct((n * EX_DEV, n_query), f32),
        in_specs=[hbm, hbm, vmem, hbm, hbm, vmem, vmem, vmem, vmem],
        out_specs=vmem,
        scratch_shapes=[
            pltpu.VMEM(activations.shape, bf16),
            pltpu.VMEM(out_grads.shape, bf16),
            pltpu.VMEM((n,) + in_factor.shape, bf16),
            pltpu.VMEM((n,) + out_factor.shape, bf16),
            pltpu.VMEM((n, rank + IDS, tokens), bf16),
            pltpu.VMEM((n, rank, tokens), bf16),
            pltpu.VMEM((rank, tokens), f32),
            pltpu.VMEM((rank, tokens), f32),
            pltpu.VMEM((n, n_query * rank, tokens), f32),
            pltpu.VMEM((n_query * rank, rank), bf16),
            pltpu.VMEM((rank, n_query, rank), f32),
            pltpu.VMEM((rank, n_query * rank), f32),
            dma((4,)),
            dma((5, 3, n)),
            dma((5, 3, n)),
            dma((n // 2, 1, n)),
            dma((n // 2, 1, n)),
            dma((3, n)),
            dma((3, n)),
            dma((1, n)),
            dma((1, n)),
        ],
        compiler_params=pltpu.CompilerParams(collective_id=0, has_side_effects=True),
    )(
        activations,
        out_grads,
        example_ids,
        in_factor,
        out_factor,
        query_grads,
        basis_in,
        basis_out,
        eigen,
    )


def solution(mesh):
    placed = (
        P(("dom", "shard"), None),
        P(("dom", "shard"), None),
        P(("dom", "shard"), None),
        P(None, "shard"),
        P(None, "shard"),
        P("shard", None),
        P(),
        P(),
        P(),
    )
    small = mesh.shape["dom"] == 2 and mesh.shape["shard"] in (8, 16)
    return jax.shard_map(
        in_one_kernel if small else with_collectives,
        mesh=mesh,
        in_specs=placed,
        out_specs=P("dom", "shard"),
        check_vma=False,
    )
```

```python
import functools

import jax
import jax.numpy as jnp
from jax import lax
from jax.experimental import pallas as pl
from jax.experimental.pallas import tpu as pltpu
from jax.sharding import PartitionSpec as P

EX_DEV = 8
MESH = pl.DeviceIdType.MESH
HIGHEST = lax.Precision.HIGHEST
NT = (((1,), (1,)), ((), ()))
SCALE = 0.00390625
IDS = 16


def precondition(query_grads, basis_in, basis_out, eigen):
    rank = basis_in.shape[0]
    grads = query_grads.reshape(-1, rank, rank)
    rotated = jnp.einsum(
        "ai,qab,bj->qij", basis_in, grads, basis_out, precision=HIGHEST
    )
    scaled = rotated / eigen
    restored = jnp.einsum(
        "ia,qab,jb->qij", basis_in, scaled, basis_out, precision=HIGHEST
    )
    return restored.reshape(grads.shape[0], -1).astype(jnp.bfloat16)


def fold_columns(features, piece):
    return lax.dot_general(features, piece, NT, preferred_element_type=jnp.float32)


def with_collectives(
    activations,
    out_grads,
    example_ids,
    in_factor,
    out_factor,
    query_grads,
    basis_in,
    basis_out,
    eigen,
):
    rank = in_factor.shape[0]
    proj_in = fold_columns(
        activations, lax.all_gather(in_factor, "shard", axis=1, tiled=True)
    ).astype(jnp.bfloat16)
    proj_out = fold_columns(
        out_grads, lax.all_gather(out_factor, "shard", axis=1, tiled=True)
    ).astype(jnp.bfloat16)
    precond = precondition(query_grads, basis_in, basis_out, eigen)
    total_examples = EX_DEV * lax.axis_size("shard")
    global_ids = example_ids[0] + lax.axis_index("shard") * EX_DEV
    query_mats = precond.reshape(-1, rank, rank)
    rows_in = lax.all_gather(proj_in, "shard", axis=0, tiled=True)
    rows_out = lax.all_gather(proj_out, "shard", axis=0, tiled=True)
    owners = lax.all_gather(global_ids, "shard", axis=0, tiled=True)
    turned = jnp.einsum("ti,qij->tqj", rows_in, query_mats, preferred_element_type=jnp.float32)
    per_token = jnp.sum(turned * rows_out.astype(jnp.float32)[:, None, :], axis=2)
    scores = jax.ops.segment_sum(per_token, owners, num_segments=total_examples)
    return scores * SCALE


def pick(value, table):
    found = jnp.int32(table[0])
    for key in range(1, len(table)):
        found = jnp.where(value == key, jnp.int32(table[key]), found)
    return found


def kernel(
    lines,
    acts_hbm,
    grads_hbm,
    ids_ref,
    fin_hbm,
    fout_hbm,
    query_ref,
    bin_ref,
    bout_ref,
    eig_ref,
    out_ref,
    acts,
    grads,
    fin,
    fout,
    rin,
    rout,
    acc_in,
    acc_out,
    turned,
    mats,
    blocks,
    wide,
    load_sem,
    send_fin,
    send_fout,
    send_rin,
    send_rout,
    recv_fin,
    recv_fout,
    recv_rin,
    recv_rout,
):
    x = lax.axis_index("dom")
    s = lax.axis_index("shard")
    z, y, c = s // 4, (s // 2) % 2, s % 2
    rank = fin.shape[1]
    half = rank // 2
    quarter = rank // 4
    n_query = query_ref.shape[0]

    def place(zz, yy, cc):
        return (zz * 2 + yy) * 2 + cc

    up = jnp.minimum(z + 1, lines - 1)
    down = jnp.maximum(z - 1, 0)
    has_up, has_down = z < lines - 1, z > 0
    dev_up, dev_down = (x, place(up, y, c)), (x, place(down, y, c))
    dev_y, dev_x, dev_core = (x, place(z, 1 - y, c)), (1 - x, s), (x, place(z, y, 1 - c))

    loads = [
        pltpu.make_async_copy(fin_hbm, fin.at[s], load_sem.at[0]),
        pltpu.make_async_copy(fout_hbm, fout.at[s], load_sem.at[1]),
        pltpu.make_async_copy(acts_hbm, acts, load_sem.at[2]),
        pltpu.make_async_copy(grads_hbm, grads, load_sem.at[3]),
    ]
    for load in loads:
        load.start()

    barrier = pltpu.get_barrier_semaphore()

    def greet(dev):
        pl.semaphore_signal(barrier, inc=1, device_id=dev, device_id_type=MESH)

    @pl.when(has_up)
    def _():
        greet(dev_up)

    @pl.when(has_down)
    def _():
        greet(dev_down)

    greet(dev_y)
    greet(dev_x)
    greet(dev_core)
    pl.semaphore_wait(
        barrier, 3 + jnp.where(has_up, 1, 0) + jnp.where(has_down, 1, 0)
    )

    stores = (fin, fout, rin, rout)
    sends = (send_fin, send_fout, send_rin, send_rout)
    recvs = (recv_fin, recv_fout, recv_rin, recv_rout)
    pending = []

    def block(f, g):
        if f >= 2:
            return 0, 0, stores[f].shape[1]
        if g == "native":
            return x, pl.multiple_of(x * quarter, quarter), quarter
        if g == "cross":
            return 1 - x, pl.multiple_of((1 - x) * quarter, quarter), quarter
        if g == "whole":
            return 3, 0, rank
        return 2, half, half

    def copy(f, g, p, kind, dev):
        slot, start, size = block(f, g)
        ref = stores[f].at[p, pl.ds(start, size)]
        return pltpu.make_async_remote_copy(
            src_ref=ref,
            dst_ref=ref,
            send_sem=sends[f].at[kind, slot, p],
            recv_sem=recvs[f].at[slot, p],
            device_id=dev,
            device_id_type=MESH,
        )

    def send(f, g, p, kind, dev, cond=None):
        make = functools.partial(copy, f, g, p, kind, dev)
        if cond is None:
            make().start()
        else:

            @pl.when(cond)
            def _():
                make().start()

        pending.append((cond, make))

    def arrive(f, g, p):
        copy(f, g, p, 0, dev_core).wait_recv()

    def along(f, g, p, zz=None):
        if zz is None:
            send(f, g, p, 0, dev_up, has_up)
            send(f, g, p, 1, dev_down, has_down)
            return
        from_below = zz < z
        dev = (x, jnp.where(from_below, dev_up[1], dev_down[1]))
        cond = jnp.where(from_below, z + 1, lines - z) < lines
        send(f, g, p, 0, dev, cond)

    def yz_first(f, g):
        return f == 0 and g == "rest"

    def own(f):
        for g in ("native", "rest"):
            along(f, g, s)
            send(f, g, s, 2, dev_y)
        send(f, "whole", s, 4, dev_core)

    near = [
        sorted([w for w in range(lines) if w != v], key=lambda w: (abs(w - v), w))
        for v in range(lines)
    ]
    others = [pick(z, [near[v][k] for v in range(lines)]) for k in range(lines - 1)]
    route = [(None, True)]
    for far in others:
        route += [(far, False), (far, True)]

    def spot(k, cc):
        far, turn = route[k]
        return place(z if far is None else far, 1 - y if turn else y, cc)

    def spread(f):
        for k in reversed(range(len(route))):
            send(f, "all", s, k, (x, spot(k, c)))
        send(f, "all", s, len(route), dev_core)

    def passed(f, k):
        p = spot(k, c)
        arrive(f, "all", p)
        send(f, "all", p, len(route), dev_core)

    def native(f, k):
        far, turn = route[k]
        p = spot(k, c)
        for g in ("native", "rest"):
            arrive(f, g, p)
            if yz_first(f, g):
                along(f, g, p, far)
            elif not turn:
                along(f, g, p, far)
                send(f, g, p, 2, dev_y)
            if g == "native":
                send(f, g, p, 3, dev_x)

    def fold(f, p):
        xs, acc = ((acts, acc_in), (grads, acc_out))[f]
        width = stores[f].shape[2]
        cols = pl.ds(pl.multiple_of(p * width, 128), width)
        acc[...] += fold_columns(stores[f][p], xs[:, cols])

    def cross(f, k):
        p = spot(k, c)
        arrive(f, "cross", p)
        send(f, "whole", p, 4, dev_core)
        fold(f, p)

    def partner(f, k):
        p = dev_core[1] if k < 0 else spot(k, 1 - c)
        arrive(f, "whole", p)
        fold(f, p)

    def turn_rows(p):
        turned[p] = jnp.dot(
            mats[...], rin[p, pl.ds(0, rank), :], preferred_element_type=jnp.float32
        )

    def finish(p):
        rows = rout[p].astype(jnp.float32)
        prod = turned[p].reshape(n_query, rank, rows.shape[1]) * rows[None]
        per_token = jnp.sum(prod, axis=1)
        ids = rin[p, pl.ds(rank, IDS), :].astype(jnp.float32)[:EX_DEV]
        want = lax.broadcasted_iota(jnp.int32, ids.shape, 0).astype(jnp.float32)
        member = jnp.where(ids == want, 1.0, 0.0).astype(jnp.bfloat16)
        high = per_token.astype(jnp.bfloat16)
        low = (per_token - high.astype(jnp.float32)).astype(jnp.bfloat16)
        total = fold_columns(member, high) + fold_columns(member, low)
        out_ref[pl.ds(pl.multiple_of(p * EX_DEV, EX_DEV), EX_DEV), :] = total * SCALE

    loads[0].wait()
    own(0)
    loads[1].wait()
    own(1)

    acc_in[...] = jnp.zeros_like(acc_in)
    acc_out[...] = jnp.zeros_like(acc_out)
    ids = jnp.broadcast_to(ids_ref[...].astype(jnp.float32), (IDS, ids_ref.shape[1]))
    rin[s, pl.ds(rank, IDS), :] = ids.astype(jnp.bfloat16)

    for a in range(rank):
        blocks[a] = query_ref[:, a * rank : (a + 1) * rank]
    first = jnp.dot(
        blocks[...].reshape(rank * n_query, rank), bout_ref[...], precision=HIGHEST
    )
    blocks[...] = first.reshape(rank, n_query, rank)
    for q in range(n_query):
        wide[:, q * rank : (q + 1) * rank] = blocks[:, q, :]
    rotated = jnp.dot(bin_ref[...].T, wide[...], precision=HIGHEST)
    wide[...] = rotated / jnp.concatenate([eig_ref[...]] * n_query, axis=1)
    wide[...] = jnp.dot(bin_ref[...], wide[...], precision=HIGHEST)
    for q in range(n_query):
        mats[q * rank : (q + 1) * rank, :] = lax.dot_general(
            bout_ref[...], wide[:, q * rank : (q + 1) * rank], NT, precision=HIGHEST,
            preferred_element_type=jnp.float32,
        ).astype(jnp.bfloat16)

    steps = len(route)
    lead, lag, slow = 1, 4, 8
    order = []
    for k in range(steps + lead):
        if k < steps:
            order.append((0, k))
        if k >= lead:
            order.append((1, k - lead))
    fold_own = {2: 0, 6: 1}

    def close(f, k):
        partner(f, k)
        if (f, k) == (0, steps - 1):
            rin[s, pl.ds(0, rank), :] = acc_in[...].astype(jnp.bfloat16)
            spread(2)

    for i in range(len(order)):
        native(*order[i])
        if i in fold_own:
            f = fold_own[i]
            loads[2 + f].wait()
            fold(f, s)
            partner(f, -1)
        if i >= lag:
            cross(*order[i - lag])
        if i >= slow:
            close(*order[i - slow])
    for i in range(len(order), len(order) + slow):
        if i - lag < len(order):
            cross(*order[i - lag])
        close(*order[i - slow])
    rout[s] = acc_out[...].astype(jnp.bfloat16)
    spread(3)
    turn_rows(s)
    for k in range(steps):
        passed(2, k)
        turn_rows(spot(k, c))
    for k in range(-1, steps):
        p = dev_core[1] if k < 0 else spot(k, 1 - c)
        arrive(2, "all", p)
        turn_rows(p)
    finish(s)
    arrive(3, "all", dev_core[1])
    finish(dev_core[1])
    for k in range(steps):
        passed(3, k)
        finish(spot(k, c))
    for k in range(steps):
        arrive(3, "all", spot(k, 1 - c))
        finish(spot(k, 1 - c))

    for cond, make in pending:
        if cond is None:
            make().wait_send()
        else:

            @pl.when(cond)
            def _(make=make):
                make().wait_send()


def in_one_kernel(
    activations,
    out_grads,
    example_ids,
    in_factor,
    out_factor,
    query_grads,
    basis_in,
    basis_out,
    eigen,
):
    n = lax.axis_size("shard")
    rank = in_factor.shape[0]
    tokens = activations.shape[0]
    n_query = query_grads.shape[0]
    bf16, f32 = jnp.bfloat16, jnp.float32
    hbm = pl.BlockSpec(memory_space=pl.ANY)
    vmem = pl.BlockSpec(memory_space=pltpu.VMEM)
    dma = pltpu.SemaphoreType.DMA
    return pl.pallas_call(
        functools.partial(kernel, n // 4),
        out_shape=jax.ShapeDtypeStruct((n * EX_DEV, n_query), f32),
        in_specs=[hbm, hbm, vmem, hbm, hbm, vmem, vmem, vmem, vmem],
        out_specs=vmem,
        scratch_shapes=[
            pltpu.VMEM(activations.shape, bf16),
            pltpu.VMEM(out_grads.shape, bf16),
            pltpu.VMEM((n,) + in_factor.shape, bf16),
            pltpu.VMEM((n,) + out_factor.shape, bf16),
            pltpu.VMEM((n, rank + IDS, tokens), bf16),
            pltpu.VMEM((n, rank, tokens), bf16),
            pltpu.VMEM((rank, tokens), f32),
            pltpu.VMEM((rank, tokens), f32),
            pltpu.VMEM((n, n_query * rank, tokens), f32),
            pltpu.VMEM((n_query * rank, rank), bf16),
            pltpu.VMEM((rank, n_query, rank), f32),
            pltpu.VMEM((rank, n_query * rank), f32),
            dma((4,)),
            dma((5, 4, n)),
            dma((5, 4, n)),
            dma((n // 2, 1, n)),
            dma((n // 2, 1, n)),
            dma((4, n)),
            dma((4, n)),
            dma((1, n)),
            dma((1, n)),
        ],
        compiler_params=pltpu.CompilerParams(collective_id=0, has_side_effects=True),
    )(
        activations,
        out_grads,
        example_ids,
        in_factor,
        out_factor,
        query_grads,
        basis_in,
        basis_out,
        eigen,
    )


def solution(mesh):
    placed = (
        P(("dom", "shard"), None),
        P(("dom", "shard"), None),
        P(("dom", "shard"), None),
        P(None, "shard"),
        P(None, "shard"),
        P("shard", None),
        P(),
        P(),
        P(),
    )
    small = mesh.shape["dom"] == 2 and mesh.shape["shard"] in (8, 16)
    return jax.shard_map(
        in_one_kernel if small else with_collectives,
        mesh=mesh,
        in_specs=placed,
        out_specs=P("dom", "shard"),
        check_vma=False,
    )
```

```python
import functools

import jax
import jax.numpy as jnp
from jax import lax
from jax.experimental import pallas as pl
from jax.experimental.pallas import tpu as pltpu
from jax.sharding import PartitionSpec as P

EX_DEV = 8
MESH = pl.DeviceIdType.MESH
HIGHEST = lax.Precision.HIGHEST
NT = (((1,), (1,)), ((), ()))
SCALE = 0.00390625
IDS = 16


def precondition(query_grads, basis_in, basis_out, eigen):
    rank = basis_in.shape[0]
    grads = query_grads.reshape(-1, rank, rank)
    rotated = jnp.einsum(
        "ai,qab,bj->qij", basis_in, grads, basis_out, precision=HIGHEST
    )
    scaled = rotated / eigen
    restored = jnp.einsum(
        "ia,qab,jb->qij", basis_in, scaled, basis_out, precision=HIGHEST
    )
    return restored.reshape(grads.shape[0], -1).astype(jnp.bfloat16)


def fold_columns(features, piece):
    return lax.dot_general(features, piece, NT, preferred_element_type=jnp.float32)


def with_collectives(
    activations,
    out_grads,
    example_ids,
    in_factor,
    out_factor,
    query_grads,
    basis_in,
    basis_out,
    eigen,
):
    rank = in_factor.shape[0]
    proj_in = fold_columns(
        activations, lax.all_gather(in_factor, "shard", axis=1, tiled=True)
    ).astype(jnp.bfloat16)
    proj_out = fold_columns(
        out_grads, lax.all_gather(out_factor, "shard", axis=1, tiled=True)
    ).astype(jnp.bfloat16)
    precond = precondition(query_grads, basis_in, basis_out, eigen)
    total_examples = EX_DEV * lax.axis_size("shard")
    global_ids = example_ids[0] + lax.axis_index("shard") * EX_DEV
    query_mats = precond.reshape(-1, rank, rank)
    rows_in = lax.all_gather(proj_in, "shard", axis=0, tiled=True)
    rows_out = lax.all_gather(proj_out, "shard", axis=0, tiled=True)
    owners = lax.all_gather(global_ids, "shard", axis=0, tiled=True)
    turned = jnp.einsum("ti,qij->tqj", rows_in, query_mats, preferred_element_type=jnp.float32)
    per_token = jnp.sum(turned * rows_out.astype(jnp.float32)[:, None, :], axis=2)
    scores = jax.ops.segment_sum(per_token, owners, num_segments=total_examples)
    return scores * SCALE


def pick(value, table):
    found = jnp.int32(table[0])
    for key in range(1, len(table)):
        found = jnp.where(value == key, jnp.int32(table[key]), found)
    return found


def kernel(
    lines,
    acts_hbm,
    grads_hbm,
    ids_ref,
    fin_hbm,
    fout_hbm,
    query_ref,
    bin_ref,
    bout_ref,
    eig_ref,
    out_ref,
    acts,
    grads,
    fin,
    fout,
    rin,
    rout,
    acc_in,
    acc_out,
    turned,
    mats,
    blocks,
    wide,
    load_sem,
    send_fin,
    send_fout,
    send_rin,
    send_rout,
    recv_fin,
    recv_fout,
    recv_rin,
    recv_rout,
):
    x = lax.axis_index("dom")
    s = lax.axis_index("shard")
    z, y, c = s // 4, (s // 2) % 2, s % 2
    rank = fin.shape[1]
    half = rank // 2
    quarter = rank // 4
    n_query = query_ref.shape[0]

    def place(zz, yy, cc):
        return (zz * 2 + yy) * 2 + cc

    up = jnp.minimum(z + 1, lines - 1)
    down = jnp.maximum(z - 1, 0)
    has_up, has_down = z < lines - 1, z > 0
    dev_up, dev_down = (x, place(up, y, c)), (x, place(down, y, c))
    dev_y, dev_x, dev_core = (x, place(z, 1 - y, c)), (1 - x, s), (x, place(z, y, 1 - c))

    loads = [
        pltpu.make_async_copy(fin_hbm, fin.at[s], load_sem.at[0]),
        pltpu.make_async_copy(fout_hbm, fout.at[s], load_sem.at[1]),
        pltpu.make_async_copy(acts_hbm, acts, load_sem.at[2]),
        pltpu.make_async_copy(grads_hbm, grads, load_sem.at[3]),
    ]
    for load in loads:
        load.start()

    barrier = pltpu.get_barrier_semaphore()

    def greet(dev):
        pl.semaphore_signal(barrier, inc=1, device_id=dev, device_id_type=MESH)

    @pl.when(has_up)
    def _():
        greet(dev_up)

    @pl.when(has_down)
    def _():
        greet(dev_down)

    greet(dev_y)
    greet(dev_x)
    greet(dev_core)
    pl.semaphore_wait(
        barrier, 3 + jnp.where(has_up, 1, 0) + jnp.where(has_down, 1, 0)
    )

    stores = (fin, fout, rin, rout)
    sends = (send_fin, send_fout, send_rin, send_rout)
    recvs = (recv_fin, recv_fout, recv_rin, recv_rout)
    pending = []

    def block(f, g):
        if f >= 2:
            return 0, 0, stores[f].shape[1]
        if g == "native":
            return x, pl.multiple_of(x * quarter, quarter), quarter
        if g == "cross":
            return 1 - x, pl.multiple_of((1 - x) * quarter, quarter), quarter
        return 2, half, half

    def copy(f, g, p, kind, dev):
        slot, start, size = block(f, g)
        ref = stores[f].at[p, pl.ds(start, size)]
        return pltpu.make_async_remote_copy(
            src_ref=ref,
            dst_ref=ref,
            send_sem=sends[f].at[kind, slot, p],
            recv_sem=recvs[f].at[slot, p],
            device_id=dev,
            device_id_type=MESH,
        )

    def send(f, g, p, kind, dev, cond=None):
        make = functools.partial(copy, f, g, p, kind, dev)
        if cond is None:
            make().start()
        else:

            @pl.when(cond)
            def _():
                make().start()

        pending.append((cond, make))

    def arrive(f, g, p):
        copy(f, g, p, 0, dev_core).wait_recv()

    def along(f, g, p, zz=None):
        if zz is None:
            send(f, g, p, 0, dev_up, has_up)
            send(f, g, p, 1, dev_down, has_down)
            return
        from_below = zz < z
        dev = (x, jnp.where(from_below, dev_up[1], dev_down[1]))
        cond = jnp.where(from_below, z + 1, lines - z) < lines
        send(f, g, p, 0, dev, cond)

    def yz_first(f, g):
        return f == 1 and g == "rest"

    def own(f):
        for g in ("native", "rest"):
            along(f, g, s)
            send(f, g, s, 2, dev_y)
        for g in ("native", "cross", "rest"):
            send(f, g, s, 4, dev_core)

    near = [
        sorted([w for w in range(lines) if w != v], key=lambda w: (abs(w - v), w))
        for v in range(lines)
    ]
    others = [pick(z, [near[v][k] for v in range(lines)]) for k in range(lines - 1)]
    route = [(None, True)]
    for far in others:
        route += [(far, False), (far, True)]

    def spot(k, cc):
        far, turn = route[k]
        return place(z if far is None else far, 1 - y if turn else y, cc)

    def spread(f):
        for k in reversed(range(len(route))):
            send(f, "all", s, k, (x, spot(k, c)))
        send(f, "all", s, len(route), dev_core)

    def passed(f, k):
        p = spot(k, c)
        arrive(f, "all", p)
        send(f, "all", p, len(route), dev_core)

    def native(f, k):
        far, turn = route[k]
        p = spot(k, c)
        for g in ("native", "rest"):
            arrive(f, g, p)
            if yz_first(f, g):
                along(f, g, p, far)
            elif not turn:
                along(f, g, p, far)
                send(f, g, p, 2, dev_y)
            if g == "native":
                send(f, g, p, 3, dev_x)
            send(f, g, p, 4, dev_core)

    def fold(f, p):
        xs, acc = ((acts, acc_in), (grads, acc_out))[f]
        width = stores[f].shape[2]
        cols = pl.ds(pl.multiple_of(p * width, 128), width)
        acc[...] += fold_columns(stores[f][p], xs[:, cols])

    def cross(f, k):
        p = spot(k, c)
        arrive(f, "cross", p)
        send(f, "cross", p, 4, dev_core)
        fold(f, p)

    def partner(f, k):
        p = dev_core[1] if k < 0 else spot(k, 1 - c)
        for g in ("native", "cross", "rest"):
            arrive(f, g, p)
        fold(f, p)

    def turn_rows(p):
        turned[p] = jnp.dot(
            mats[...], rin[p, pl.ds(0, rank), :], preferred_element_type=jnp.float32
        )

    def finish(p):
        rows = rout[p].astype(jnp.float32)
        prod = turned[p].reshape(n_query, rank, rows.shape[1]) * rows[None]
        per_token = jnp.sum(prod, axis=1)
        ids = rin[p, pl.ds(rank, IDS), :].astype(jnp.float32)[:EX_DEV]
        want = lax.broadcasted_iota(jnp.int32, ids.shape, 0).astype(jnp.float32)
        member = jnp.where(ids == want, 1.0, 0.0).astype(jnp.bfloat16)
        high = per_token.astype(jnp.bfloat16)
        low = (per_token - high.astype(jnp.float32)).astype(jnp.bfloat16)
        total = fold_columns(member, high) + fold_columns(member, low)
        out_ref[pl.ds(pl.multiple_of(p * EX_DEV, EX_DEV), EX_DEV), :] = total * SCALE

    loads[0].wait()
    own(0)
    loads[1].wait()
    own(1)

    acc_in[...] = jnp.zeros_like(acc_in)
    acc_out[...] = jnp.zeros_like(acc_out)
    ids = jnp.broadcast_to(ids_ref[...].astype(jnp.float32), (IDS, ids_ref.shape[1]))
    rin[s, pl.ds(rank, IDS), :] = ids.astype(jnp.bfloat16)

    for a in range(rank):
        blocks[a] = query_ref[:, a * rank : (a + 1) * rank]
    first = jnp.dot(
        blocks[...].reshape(rank * n_query, rank), bout_ref[...], precision=HIGHEST
    )
    blocks[...] = first.reshape(rank, n_query, rank)
    for q in range(n_query):
        wide[:, q * rank : (q + 1) * rank] = blocks[:, q, :]
    rotated = jnp.dot(bin_ref[...].T, wide[...], precision=HIGHEST)
    wide[...] = rotated / jnp.concatenate([eig_ref[...]] * n_query, axis=1)
    wide[...] = jnp.dot(bin_ref[...], wide[...], precision=HIGHEST)
    for q in range(n_query):
        mats[q * rank : (q + 1) * rank, :] = lax.dot_general(
            bout_ref[...], wide[:, q * rank : (q + 1) * rank], NT, precision=HIGHEST,
            preferred_element_type=jnp.float32,
        ).astype(jnp.bfloat16)

    steps = len(route)
    lead, lag, slow = 1, 4, 8
    order = []
    for k in range(steps + lead):
        if k < steps:
            order.append((0, k))
        if k >= lead:
            order.append((1, k - lead))
    fold_own = {2: 0, 6: 1}

    def close(f, k):
        partner(f, k)
        if (f, k) == (0, steps - 1):
            rin[s, pl.ds(0, rank), :] = acc_in[...].astype(jnp.bfloat16)
            spread(2)

    for i in range(len(order)):
        native(*order[i])
        if i in fold_own:
            f = fold_own[i]
            loads[2 + f].wait()
            fold(f, s)
            partner(f, -1)
        if i >= lag:
            cross(*order[i - lag])
        if i >= slow:
            close(*order[i - slow])
    for i in range(len(order), len(order) + slow):
        if i - lag < len(order):
            cross(*order[i - lag])
        close(*order[i - slow])
    rout[s] = acc_out[...].astype(jnp.bfloat16)
    spread(3)
    turn_rows(s)
    for k in range(steps):
        passed(2, k)
        turn_rows(spot(k, c))
    for k in range(-1, steps):
        p = dev_core[1] if k < 0 else spot(k, 1 - c)
        arrive(2, "all", p)
        turn_rows(p)
    finish(s)
    arrive(3, "all", dev_core[1])
    finish(dev_core[1])
    for k in range(steps):
        passed(3, k)
        finish(spot(k, c))
    for k in range(steps):
        arrive(3, "all", spot(k, 1 - c))
        finish(spot(k, 1 - c))

    for cond, make in pending:
        if cond is None:
            make().wait_send()
        else:

            @pl.when(cond)
            def _(make=make):
                make().wait_send()


def in_one_kernel(
    activations,
    out_grads,
    example_ids,
    in_factor,
    out_factor,
    query_grads,
    basis_in,
    basis_out,
    eigen,
):
    n = lax.axis_size("shard")
    rank = in_factor.shape[0]
    tokens = activations.shape[0]
    n_query = query_grads.shape[0]
    bf16, f32 = jnp.bfloat16, jnp.float32
    hbm = pl.BlockSpec(memory_space=pl.ANY)
    vmem = pl.BlockSpec(memory_space=pltpu.VMEM)
    dma = pltpu.SemaphoreType.DMA
    return pl.pallas_call(
        functools.partial(kernel, n // 4),
        out_shape=jax.ShapeDtypeStruct((n * EX_DEV, n_query), f32),
        in_specs=[hbm, hbm, vmem, hbm, hbm, vmem, vmem, vmem, vmem],
        out_specs=vmem,
        scratch_shapes=[
            pltpu.VMEM(activations.shape, bf16),
            pltpu.VMEM(out_grads.shape, bf16),
            pltpu.VMEM((n,) + in_factor.shape, bf16),
            pltpu.VMEM((n,) + out_factor.shape, bf16),
            pltpu.VMEM((n, rank + IDS, tokens), bf16),
            pltpu.VMEM((n, rank, tokens), bf16),
            pltpu.VMEM((rank, tokens), f32),
            pltpu.VMEM((rank, tokens), f32),
            pltpu.VMEM((n, n_query * rank, tokens), f32),
            pltpu.VMEM((n_query * rank, rank), bf16),
            pltpu.VMEM((rank, n_query, rank), f32),
            pltpu.VMEM((rank, n_query * rank), f32),
            dma((4,)),
            dma((5, 3, n)),
            dma((5, 3, n)),
            dma((n // 2, 1, n)),
            dma((n // 2, 1, n)),
            dma((3, n)),
            dma((3, n)),
            dma((1, n)),
            dma((1, n)),
        ],
        compiler_params=pltpu.CompilerParams(collective_id=0, has_side_effects=True),
    )(
        activations,
        out_grads,
        example_ids,
        in_factor,
        out_factor,
        query_grads,
        basis_in,
        basis_out,
        eigen,
    )


def solution(mesh):
    placed = (
        P(("dom", "shard"), None),
        P(("dom", "shard"), None),
        P(("dom", "shard"), None),
        P(None, "shard"),
        P(None, "shard"),
        P("shard", None),
        P(),
        P(),
        P(),
    )
    small = mesh.shape["dom"] == 2 and mesh.shape["shard"] in (8, 16)
    return jax.shard_map(
        in_one_kernel if small else with_collectives,
        mesh=mesh,
        in_specs=placed,
        out_specs=P("dom", "shard"),
        check_vma=False,
    )
```
